256 devices in a mesh: rows: 16 (over y, x_hi, core), feat: 16 (over z, x_lo).
Axes of the slice: x: 4 (x_hi: 2, x_lo: 2; x = x_hi * 2 + x_lo), y: 4, z: 8, core: 2. Of those that a mesh axis runs over, the one named last changes fastest.
Arguments:
- inputs: bfloat16 [32768, 512], P('rows'), may hold values from -6 to 6
- weight: bfloat16 [512, 32768], P(None, 'feat'), may hold values from -1.25 to 1.25
- phases: float32 [32768], P('feat'), may hold values from -3.140625 to 3.140625
- labels: int32 [32768], P('rows'), may hold values from 0 to 2047
- prediction: bfloat16 [32768, 2048], P('rows', 'feat'), may hold values from -4 to 4
- ridge_inverse: float32 [32768, 2048], P(('feat', 'rows')), may hold values from -2 to 2, as said below
- coefficients: float32 [32768, 2048], P(('feat', 'rows')), may hold values from -6 to 6
Outputs:
- coefficients_out: float32 [32768, 2048], P(('feat', 'rows'))
- residual_out: float32 [32768, 2048], P('rows', 'feat')
The draws below stay inside these ranges and needn't reach their ends.
Inputs may be any that keep to these rules, and one draw needn't show every extreme that they name: `ridge_inverse`: each M_b is symmetric and positive definite.
All inputs are finite; a program needn't handle non-finite values.
Results may differ from the reference program's by a relative error of at most 0.003.
Values may be sent and summed in bfloat16 or wider, within the bound.
A program may use at most 64 MiB of HBM per device.

```python
import math
import jax
import jax.numpy as jnp
from jax import lax

DIN = 512
FB = 2048
PANEL = 128
TICKS = 4
TOTAL_ROWS = 32768
FEATURES = 32768
CLASSES = 2048
N_FEAT = 16


def draw_ridge_inverse(key, part):
    blocks_count = FEATURES // FB
    noise = jnp.clip(jax.random.normal(key, (blocks_count, FB, FB), jnp.float32), -5.0, 5.0)
    symmetric = noise + jnp.transpose(noise, (0, 2, 1))
    matrix = jnp.eye(FB, dtype=jnp.float32)[None] + 0.25 * symmetric / jnp.sqrt(jnp.float32(FB))
    return matrix.reshape(FEATURES, FB).astype(jnp.float32)


def with_ends(drawn, rng, smallest, top_value):
    index_at = [jax.random.randint(jax.random.fold_in(rng, axis), (), 0, length) for axis, length in enumerate(drawn.shape)]
    widest = drawn.shape.index(max(drawn.shape))
    neighbour = index_at[:widest] + [(index_at[widest] + 1) % drawn.shape[widest]] + index_at[widest + 1:]
    return drawn.at[tuple(index_at)].set(smallest).at[tuple(neighbour)].set(top_value)


def shard_levels(key, dims, pieces, low, high):
    def one(dim, shards_of):
        heights = jax.random.uniform(jax.random.fold_in(jax.random.fold_in(key, 6), dim), (shards_of,), jnp.float32, low / len(pieces), high / len(pieces))
        return jnp.repeat(jnp.exp(heights), dims[dim] // shards_of).reshape((-1,) + (1,) * (len(dims) - dim - 1))

    factor_of = one(*pieces[0])
    for cut in pieces[1:]:
        factor_of = factor_of * one(*cut)
    return factor_of


def normal_values(own_key, extent, spread, bound, pieces=(), held_as=jnp.bfloat16):
    values = spread * jax.random.normal(own_key, extent, jnp.float32)
    if pieces:
        values = values * shard_levels(own_key, extent, pieces, -0.22, 0.18)
    return jnp.clip(values, -bound, bound).astype(held_as)


def setup_inputs(seed: int = 0) -> dict:
    keys = jax.random.split(jax.random.key(seed), 8)
    return {
        "inputs": normal_values(keys[0], (TOTAL_ROWS, DIN), 1.0, 6.0, ((0, 16),)),
        "weight": normal_values(keys[1], (DIN, FEATURES), (DIN // 25) ** -0.5, 1.25, ((1, 16),)),
        "phases": jnp.clip(jax.random.uniform(keys[2], (FEATURES,), jnp.float32, -3.140625, 3.140625), -3.140625, 3.140625),
        "labels": with_ends(jax.random.randint(keys[3], (TOTAL_ROWS,), 0, CLASSES), jax.random.fold_in(keys[3], 1), 0, CLASSES - 1).astype(jnp.int32),
        "prediction": normal_values(keys[4], (TOTAL_ROWS, CLASSES), 0.5, 4.0, ((0, 16), (1, 16))),
        "ridge_inverse": draw_ridge_inverse(jax.random.fold_in(keys[7], 71), 0),
        "coefficients": normal_values(keys[6], (FEATURES, CLASSES), 1.0, 6.0, ((0, 256),), jnp.float32),
    }


ridge_weight = 0.5

def reference(inputs, weight, phases, labels, prediction, ridge_inverse, coefficients):
    scale = 1.0 / math.sqrt(TOTAL_ROWS)
    blocks = []
    for b in range(N_FEAT):
        linear = jnp.dot(inputs, weight[:, b * FB:(b + 1) * FB], preferred_element_type=jnp.float32) + phases[b * FB:(b + 1) * FB]
        blocks.append((jnp.cos(linear) * scale).astype(jnp.bfloat16))
    target = (labels[:, None] == jnp.arange(CLASSES, dtype=jnp.int32)[None, :]).astype(jnp.float32)
    residual = target - prediction.astype(jnp.float32)
    panels = [residual[:, q * PANEL:(q + 1) * PANEL] for q in range(N_FEAT)]
    coeffs = coefficients
    for tick in range(TICKS):
        for q in range(N_FEAT):
            b = (q + tick) % N_FEAT
            feature_block = blocks[b]
            correlation = jnp.dot(feature_block.T, panels[q].astype(jnp.bfloat16), preferred_element_type=jnp.float32)
            earlier = coeffs[b * FB:(b + 1) * FB, q * PANEL:(q + 1) * PANEL]
            right_side = correlation - ridge_weight * earlier
            change = jnp.dot(ridge_inverse[b * FB:(b + 1) * FB], right_side, precision=lax.Precision.HIGHEST, preferred_element_type=jnp.float32)
            coeffs = coeffs.at[b * FB:(b + 1) * FB, q * PANEL:(q + 1) * PANEL].set(earlier + change)
            panels[q] = panels[q] - jnp.dot(feature_block, change.astype(jnp.bfloat16), preferred_element_type=jnp.float32)
    ordered = [panels[(j - TICKS) % N_FEAT] for j in range(N_FEAT)]
    return (coeffs, jnp.concatenate(ordered, axis=1))
```

```python
import functools
import math

import jax
import jax.numpy as jnp
from jax import lax
from jax.experimental import pallas as pl
from jax.experimental.pallas import tpu as pltpu
from jax.sharding import PartitionSpec as P

TICKS = 4
RIDGE = 0.5
HALVES = 2

COS_POLY = (
    0.9999999890590228,
    -19.739204499453827,
    64.9391174598908,
    -85.45013953079768,
    60.16763095026347,
    -25.967599245923736,
    6.52865815775625,
)
INV_TURN = 1.0 / (2.0 * math.pi)

RS, AG1, AG2, HOP = range(4)


def nt(a, b):
    return lax.dot_general(a, b, (((1,), (1,)), ((), ())), preferred_element_type=jnp.float32)


def kernel(
    n_rows, n_feat, scale,
    x_ref, w_ref, ph_ref, lab_ref, pred_ref, m_ref, c_ref,
    cout_ref, rout_ref,
    feat, preds, dsum, rt, rs_out, rs_in, ag1, ag2, change, mcat, ct,
    send, recv, psend, precv,
):
    me = lax.axis_index("rows")
    fi = lax.axis_index("feat")
    width = pred_ref.shape[1]
    rows = x_ref.shape[0]
    fb = w_ref.shape[1]
    strip = m_ref.shape[0]
    hw = width // HALVES
    nxt = lax.rem(fi + 1, n_feat)

    barrier = pltpu.get_barrier_semaphore()

    def greet(k, _):
        pl.semaphore_signal(barrier, inc=1, device_id=(lax.rem(me + k, n_rows), fi))
        return 0

    lax.fori_loop(1, n_rows, greet, 0)
    for k in range(1, TICKS + 1):
        pl.semaphore_signal(barrier, inc=1, device_id=(me, lax.rem(fi + k, n_feat)))
        pl.semaphore_signal(barrier, inc=1, device_id=(me, lax.rem(fi + n_feat - k, n_feat)))
    pl.semaphore_wait(barrier, n_rows - 1 + 2 * TICKS)

    def turn(i, _):
        at = pl.ds(pl.multiple_of(i * 256, 256), 256)
        preds[0, :, at] = pred_ref[at, :].astype(jnp.float32).T.astype(jnp.bfloat16)
        return 0

    lax.fori_loop(0, rows // 256, turn, 0)

    def pred_copy(k):
        return pltpu.make_async_remote_copy(
            src_ref=preds.at[0],
            dst_ref=preds.at[k],
            send_sem=psend.at[k],
            recv_sem=precv.at[k],
            device_id=(me, lax.rem(fi + k, n_feat)),
        )

    for k in range(1, TICKS + 1):
        pred_copy(k).start()

    tr, tc = 256, 512

    def featurise(i, _):
        r0 = pl.ds(pl.multiple_of((i // (fb // tc)) * tr, tr), tr)
        c0 = pl.ds(pl.multiple_of(lax.rem(i, fb // tc) * tc, tc), tc)
        linear = jnp.dot(x_ref[r0, :], w_ref[:, c0], preferred_element_type=jnp.float32)
        turns = (linear + ph_ref[:, c0]) * INV_TURN
        part = turns - jnp.floor(turns + 0.5)
        u = part * part
        acc = u * (COS_POLY[-1] * scale) + COS_POLY[-2] * scale
        for a in COS_POLY[-3::-1]:
            acc = acc * u + a * scale
        feat[r0, c0] = acc.astype(jnp.bfloat16)
        return 0

    lax.fori_loop(0, (rows // tr) * (fb // tc), featurise, 0)

    high = m_ref[...].astype(jnp.bfloat16)
    mcat[0:strip, :] = high
    mcat[strip : 2 * strip, :] = (m_ref[...] - high.astype(jnp.float32)).astype(jnp.bfloat16)

    cout_ref[...] = c_ref[...]
    dsum[0] = jnp.zeros_like(dsum[0])

    def panel_columns(t):
        q = lax.rem(fi - t + n_feat, n_feat)
        return pl.ds(pl.multiple_of(q * width, width), width)

    def residual(t, h, j):
        q = lax.rem(fi - t + n_feat, n_feat)
        at = pl.ds(pl.multiple_of(j * 256, 256), 256)
        cls = lax.broadcasted_iota(jnp.int32, (hw, 256), 0) + (h * hw + q * width)
        hot = (lab_ref[:, at] == cls).astype(jnp.float32)
        return hot - preds[t, h * hw : (h + 1) * hw, at].astype(jnp.float32) - dsum[t, h, j].astype(jnp.float32)

    def gathered(buf, kind, t, h):
        return pltpu.make_async_remote_copy(
            src_ref=buf.at[t, h, pl.ds(0, n_rows - 1)],
            dst_ref=buf.at[t, h, pl.ds(0, n_rows - 1)],
            send_sem=send.at[kind, t, h],
            recv_sem=recv.at[kind, t, h],
            device_id=(lax.rem(me + 1, n_rows), fi),
        )

    def spread(buf, kind, t, h):
        def one(k, _):
            pltpu.make_async_remote_copy(
                src_ref=buf.at[t, h, me],
                dst_ref=buf.at[t, h, me],
                send_sem=send.at[kind, t, h],
                recv_sem=recv.at[kind, t, h],
                device_id=(lax.rem(me + k, n_rows), fi),
            ).start()
            return 0

        lax.fori_loop(1, n_rows, one, 0)

    def hop(t, h):
        return pltpu.make_async_remote_copy(
            src_ref=change.at[t, h],
            dst_ref=dsum.at[t + 1, h],
            send_sem=send.at[HOP, t, h],
            recv_sem=recv.at[HOP, t, h],
            device_id=(me, nxt),
        )

    def tick(t, _):
        ct[...] = c_ref[:, panel_columns(t)].T

        @pl.when(t > 0)
        def _():
            pred_copy(t).wait_recv()

        for h in range(HALVES):

            @pl.when(t > 0)
            def _():
                hop(t - 1, h).wait_recv()

            def fill(j, _):
                at = pl.ds(pl.multiple_of(j * 256, 256), 256)
                rt[h, :, at] = residual(t, h, j).astype(jnp.bfloat16)
                return 0

            lax.fori_loop(0, rows // 256, fill, 0)

            def correlate(k, _):
                pair = lax.rem(me // 2 + k, n_rows // 2)
                at = pl.ds(pl.multiple_of(pair * 2 * strip, 2 * strip), 2 * strip)
                part = jnp.dot(rt[h], feat[:, at], preferred_element_type=jnp.float32).astype(jnp.bfloat16)
                for j in range(2):
                    d = 2 * pair + j
                    rs_out[t, h, d] = part[:, j * strip : (j + 1) * strip]

                    @pl.when(d != me)
                    def _():
                        pltpu.make_async_remote_copy(
                            src_ref=rs_out.at[t, h, d],
                            dst_ref=rs_in.at[t, h, me],
                            send_sem=send.at[RS, t, h],
                            recv_sem=recv.at[RS, t, h],
                            device_id=(d, fi),
                        ).start()

                return 0

            lax.fori_loop(1, n_rows // 2 + 1, correlate, 0)
            rs_in[t, h, me] = rs_out[t, h, me]

        for h in range(HALVES):
            gathered(rs_in, RS, t, h).wait_recv()
            lanes = slice(h * hw, (h + 1) * hw)
            total = -RIDGE * ct[lanes, :]
            for s in range(n_rows):
                total = total + rs_in[t, h, s].astype(jnp.float32)
            ag1[t, h, me] = total.astype(jnp.bfloat16)
            spread(ag1, AG1, t, h)

        for h in range(HALVES):
            gathered(ag1, AG1, t, h).wait_recv()
            lanes = slice(h * hw, (h + 1) * hw)
            right = jnp.concatenate([ag1[t, h, s] for s in range(n_rows)], axis=1)
            both = nt(right, mcat[...])
            own = both[:, :strip] + both[:, strip:]
            ag2[t, h, me] = own.astype(jnp.bfloat16)
            spread(ag2, AG2, t, h)
            ct[lanes, :] = ct[lanes, :] + own

        cout_ref[:, panel_columns(t)] = ct[...].T

        for h in range(HALVES):
            gathered(ag2, AG2, t, h).wait_recv()
            delta = jnp.concatenate([ag2[t, h, s] for s in range(n_rows)], axis=1)

            def update(j, _):
                at = pl.ds(pl.multiple_of(j * 256, 256), 256)
                moved = nt(delta, feat[at, :])
                change[t, h, j] = (dsum[t, h, j].astype(jnp.float32) + moved).astype(jnp.bfloat16)
                pltpu.make_async_remote_copy(
                    src_ref=change.at[t, h, j],
                    dst_ref=dsum.at[t + 1, h, j],
                    send_sem=send.at[HOP, t, h],
                    recv_sem=recv.at[HOP, t, h],
                    device_id=(me, nxt),
                ).start()
                return 0

            lax.fori_loop(0, rows // 256, update, 0)
        return 0

    lax.fori_loop(0, TICKS, tick, 0)

    pred_copy(TICKS).wait_recv()
    for h in range(HALVES):
        hop(TICKS - 1, h).wait_recv()

    def finish(j, _):
        at = pl.ds(pl.multiple_of(j * 256, 256), 256)
        parts = [residual(TICKS, h, j) for h in range(HALVES)]
        rout_ref[at, :] = jnp.concatenate(parts, axis=0).T
        return 0

    lax.fori_loop(0, rows // 256, finish, 0)

    for k in range(1, TICKS + 1):
        pred_copy(k).wait_send()

    def drain(t, _):
        for h in range(HALVES):
            gathered(rs_out, RS, t, h).wait_send()
            gathered(ag1, AG1, t, h).wait_send()
            gathered(ag2, AG2, t, h).wait_send()
            hop(t, h).wait_send()
        return 0

    lax.fori_loop(0, TICKS, drain, 0)


def on_device(inputs, weight, phases, labels, prediction, ridge_inverse, coefficients):
    n_rows = lax.axis_size("rows")
    n_feat = lax.axis_size("feat")
    rows = inputs.shape[0]
    fb = weight.shape[1]
    width = prediction.shape[1]
    strip = ridge_inverse.shape[0]
    hw = width // HALVES
    scale = 1.0 / math.sqrt(rows * n_rows)
    bf = jnp.bfloat16
    vmem = pl.BlockSpec(memory_space=pltpu.VMEM)
    pieces = (TICKS, HALVES, n_rows, hw, strip)
    return pl.pallas_call(
        functools.partial(kernel, n_rows, n_feat, scale),
        out_shape=(
            jax.ShapeDtypeStruct(coefficients.shape, jnp.float32),
            jax.ShapeDtypeStruct(prediction.shape, jnp.float32),
        ),
        in_specs=[vmem] * 7,
        out_specs=(vmem, vmem),
        scratch_shapes=[
            pltpu.VMEM((rows, fb), bf),
            pltpu.VMEM((TICKS + 1, width, rows), bf),
            pltpu.VMEM((TICKS + 1, HALVES, rows // 256, hw, 256), bf),
            pltpu.VMEM((HALVES, hw, rows), bf),
            pltpu.VMEM(pieces, bf),
            pltpu.VMEM(pieces, bf),
            pltpu.VMEM(pieces, bf),
            pltpu.VMEM(pieces, bf),
            pltpu.VMEM((TICKS, HALVES, rows // 256, hw, 256), bf),
            pltpu.VMEM((2 * strip, fb), bf),
            pltpu.VMEM((width, strip), jnp.float32),
            pltpu.SemaphoreType.DMA((4, TICKS, HALVES)),
            pltpu.SemaphoreType.DMA((4, TICKS, HALVES)),
            pltpu.SemaphoreType.DMA((TICKS + 1,)),
            pltpu.SemaphoreType.DMA((TICKS + 1,)),
        ],
        compiler_params=pltpu.CompilerParams(
            collective_id=0, has_side_effects=True, vmem_limit_bytes=60 * 2**20
        ),
    )(
        inputs,
        weight,
        phases.reshape(1, -1),
        labels.reshape(1, -1),
        prediction,
        ridge_inverse,
        coefficients,
    )


def solution(mesh):
    placed = (
        P("rows", None),
        P(None, "feat"),
        P("feat"),
        P("rows"),
        P("rows", "feat"),
        P(("feat", "rows"), None),
        P(("feat", "rows"), None),
    )
    return jax.shard_map(
        on_device,
        mesh=mesh,
        in_specs=placed,
        out_specs=(P(("feat", "rows"), None), P("rows", "feat")),
        check_vma=False,
    )
```

```python
import functools
import math

import jax
import jax.numpy as jnp
from jax import lax
from jax.experimental import pallas as pl
from jax.experimental.pallas import tpu as pltpu
from jax.sharding import PartitionSpec as P

TICKS = 4
RIDGE = 0.5
HALVES = 2
CHUNKS = 8

COS_POLY = (
    0.9999999890590228,
    -19.739204499453827,
    64.9391174598908,
    -85.45013953079768,
    60.16763095026347,
    -25.967599245923736,
    6.52865815775625,
)
INV_TURN = 1.0 / (2.0 * math.pi)

RS, RIGHT, AG = range(3)


def nt(a, b):
    return lax.dot_general(a, b, (((1,), (1,)), ((), ())), preferred_element_type=jnp.float32)


def kernel(
    n_rows, n_feat, n_y, scale,
    x_ref, w_ref, ph_ref, lab_ref, pred_ref, m_ref, c_ref,
    cout_ref, rout_ref,
    feat, preds, dsum, acc, rs_out, rs_in, right, ag, change, mcat, ctn,
    send, recv, hsend, hrecv, psend, precv, msend, mrecv,
):
    me = lax.axis_index("rows")
    fi = lax.axis_index("feat")
    n_b = n_rows // n_y
    my_y = me // n_b
    my_b = lax.rem(me, n_b)
    sibling = me + 1 - 2 * lax.rem(me, 2)
    core = lax.rem(me, 2)
    chip = me // 2
    n_chip = n_rows // 2
    width = pred_ref.shape[1]
    rows = x_ref.shape[0]
    fb = w_ref.shape[1]
    strip = m_ref.shape[0]
    hw = width // HALVES
    cw = hw // 2
    block = fb // n_chip
    chunk = rows // CHUNKS
    nxt = lax.rem(fi + 1, n_feat)

    offsets = [(dy, db) for dy in (2, 1, 3, 0) for db in (2, 3, 1, 0)]

    def place(dy, db):
        return lax.rem(my_y + dy, n_y) * n_b + lax.rem(my_b + db, n_b)

    barrier = pltpu.get_barrier_semaphore()
    for dy, db in offsets[:-1]:
        pl.semaphore_signal(barrier, inc=1, device_id=(place(dy, db), fi))
    for k in (1, 2):
        pl.semaphore_signal(barrier, inc=1, device_id=(me, lax.rem(fi + k, n_feat)))
        pl.semaphore_signal(barrier, inc=1, device_id=(me, lax.rem(fi + n_feat - k, n_feat)))
    pl.semaphore_wait(barrier, n_rows - 1 + 4)

    own_rows = pl.ds(pl.multiple_of(core * strip, strip), strip)
    high = m_ref[...].astype(jnp.bfloat16)
    mcat[0, own_rows, :] = high
    mcat[1, own_rows, :] = (m_ref[...] - high.astype(jnp.float32)).astype(jnp.bfloat16)
    ridge_copy = pltpu.make_async_remote_copy(
        src_ref=mcat.at[:, own_rows],
        dst_ref=mcat.at[:, own_rows],
        send_sem=msend,
        recv_sem=mrecv,
        device_id=(sibling, fi),
    )
    ridge_copy.start()

    def turn(i, _):
        at = pl.ds(pl.multiple_of(i * 256, 256), 256)
        preds[0, :, at] = pred_ref[at, :].astype(jnp.float32).T.astype(jnp.bfloat16)
        return 0

    lax.fori_loop(0, rows // 256, turn, 0)

    def pred_copy(k):
        return pltpu.make_async_remote_copy(
            src_ref=preds.at[max(k - 2, 0)],
            dst_ref=preds.at[k],
            send_sem=psend.at[k],
            recv_sem=precv.at[k],
            device_id=(me, lax.rem(fi + min(k, 2), n_feat)),
        )

    pred_copy(1).start()
    pred_copy(2).start()

    tc = 256

    def featurise(i, _):
        c0 = pl.ds(pl.multiple_of(i * tc, tc), tc)
        linear = jnp.dot(x_ref[...], w_ref[:, c0], preferred_element_type=jnp.float32)
        turns = linear * INV_TURN + ph_ref[:, c0] * INV_TURN
        part = turns - jnp.round(turns)
        u = part * part
        value = u * (COS_POLY[-1] * scale) + COS_POLY[-2] * scale
        for a in COS_POLY[-3::-1]:
            value = value * u + a * scale
        feat[:, c0] = value.astype(jnp.bfloat16)
        return 0

    lax.fori_loop(0, fb // tc, featurise, 0)

    dsum[0] = jnp.zeros_like(dsum[0])

    def panel(t):
        return lax.rem(fi - t + n_feat, n_feat)

    def panel_columns(t):
        return pl.ds(pl.multiple_of(panel(t) * width, width), width)

    def residual(t, h, j):
        at = pl.ds(pl.multiple_of(j * chunk, chunk), chunk)
        cls = lax.broadcasted_iota(jnp.int32, (hw, chunk), 0) + (h * hw + panel(t) * width)
        hot = (lab_ref[:, at] == cls).astype(jnp.float32)
        return hot - preds[t, h * hw : (h + 1) * hw, at].astype(jnp.float32) - dsum[t, h, j].astype(jnp.float32)

    def to_place(kind, t, h, src, dst, device):
        return pltpu.make_async_remote_copy(
            src_ref=src,
            dst_ref=dst,
            send_sem=send.at[kind, t, h],
            recv_sem=recv.at[kind, t, h],
            device_id=(device, fi),
        )

    def all_of(kind, t, h, buf, count):
        some = buf.at[t, h, pl.ds(0, count)]
        return to_place(kind, t, h, some, some, sibling)

    def hop(t, h, j):
        return pltpu.make_async_remote_copy(
            src_ref=change.at[t, h, j],
            dst_ref=dsum.at[t + 1, h, j],
            send_sem=hsend.at[t, h, j],
            recv_sem=hrecv.at[t, h, j],
            device_id=(me, nxt),
        )

    def correlate(t, h):
        acc[...] = jnp.zeros_like(acc)
        cols = panel_columns(t)
        mine = pl.ds(pl.multiple_of(me * strip, strip), strip)
        acc[:, mine] = -RIDGE * c_ref[:, cols].T[h * hw : (h + 1) * hw, :]

        def arrived(j):
            @pl.when(t > 0)
            def _():
                hop(t - 1, h, j).wait_recv()

            return residual(t, h, j).astype(jnp.bfloat16)

        def first(j, _):
            part = arrived(j)
            r0 = pl.ds(pl.multiple_of(j * chunk, chunk), chunk)
            acc[...] = acc[...] + jnp.dot(part, feat[r0, :], preferred_element_type=jnp.float32)
            return 0

        lax.fori_loop(0, CHUNKS - 1, first, 0)
        last = arrived(CHUNKS - 1)
        for dy in (2, 1, 3, 0):
            y = lax.rem(my_y + dy, n_y)
            c0 = pl.ds(pl.multiple_of(y * 2 * block, 2 * block), 2 * block)
            total = acc[:, c0] + jnp.dot(
                last, feat[rows - chunk : rows, c0], preferred_element_type=jnp.float32
            )
            total = total.astype(jnp.bfloat16)
            for b in range(n_b):
                lanes = slice(b // 2 * block, (b // 2 + 1) * block)
                rs_out[t, h, y * n_b + b] = total[b % 2 * cw : (b % 2 + 1) * cw, lanes]
            for db in (2, 3, 1, 0):
                if (dy, db) != (0, 0):
                    d = place(dy, db)
                    to_place(RS, t, h, rs_out.at[t, h, d], rs_in.at[t, h, me], d).start()
        rs_in[t, h, me] = rs_out[t, h, me]

    def collect(t, h):
        all_of(RS, t, h, rs_in, n_rows - 1).wait_recv()
        total = rs_in[t, h, 0].astype(jnp.float32)
        for s in range(1, n_rows):
            total = total + rs_in[t, h, s].astype(jnp.float32)
        right[t, h, chip] = total.astype(jnp.bfloat16)
        for dy, db in offsets[:-1]:
            if db % 2 == 0:
                mine = right.at[t, h, chip]
                to_place(RIGHT, t, h, mine, mine, place(dy, db)).start()

    def solve(t, h):
        all_of(RIGHT, t, h, right, n_chip - 1).wait_recv()
        whole = jnp.concatenate([right[t, h, a] for a in range(n_chip)], axis=1)
        own = nt(whole, mcat[0]) + nt(whole, mcat[1])
        ag[t, h, me] = own.astype(jnp.bfloat16)
        for dy, db in offsets[:-1]:
            to_place(AG, t, h, ag.at[t, h, me], ag.at[t, h, me], place(dy, db)).start()

    def update(t, h):
        all_of(AG, t, h, ag, n_rows - 1).wait_recv()
        delta = jnp.concatenate(
            [
                jnp.concatenate([ag[t, h, 2 * a + c] for a in range(n_chip)], axis=1)
                for c in range(2)
            ],
            axis=0,
        )

        def moved(j, _):
            at = pl.ds(pl.multiple_of(j * chunk, chunk), chunk)
            total = dsum[t, h, j].astype(jnp.float32) + nt(delta, feat[at, :])
            change[t, h, j] = total.astype(jnp.bfloat16)
            hop(t, h, j).start()
            return 0

        lax.fori_loop(0, CHUNKS, moved, 0)
        for c in range(2):
            lanes = slice(h * hw + c * cw, h * hw + (c + 1) * cw)
            ctn[t, lanes, :] = ag[t, h, 2 * chip + c, :, own_rows].astype(jnp.float32)

    correlate(0, 0)
    correlate(0, 1)
    ridge_copy.wait_recv()
    pred_copy(1).wait_recv()
    pred_copy(3).start()

    def tick(t, _):
        for h in range(HALVES):
            collect(t, h)
        for h in range(HALVES):
            solve(t, h)

        @pl.when(t == 1)
        def _():
            pred_copy(2).wait_recv()
            pred_copy(4).start()

        for h in range(HALVES):
            update(t, h)

        @pl.when(t == 2)
        def _():
            pred_copy(3).wait_recv()

        @pl.when(t < TICKS - 1)
        def _():
            for h in range(HALVES):
                correlate(t + 1, h)

        return 0

    lax.fori_loop(0, TICKS, tick, 0)

    for t in range(TICKS):
        cols = panel_columns(t)
        if t == 0:
            cout_ref[...] = c_ref[...]
        cout_ref[:, cols] = c_ref[:, cols] + ctn[t].T

    pred_copy(TICKS).wait_recv()

    for j in range(CHUNKS):
        for h in range(HALVES):
            hop(TICKS - 1, h, j).wait_recv()
        parts = [residual(TICKS, h, j) for h in range(HALVES)]
        rout_ref[j * chunk : (j + 1) * chunk, :] = jnp.concatenate(parts, axis=0).T

    for k in range(1, TICKS + 1):
        pred_copy(k).wait_send()
    ridge_copy.wait_send()

    def drain(t, _):
        for h in range(HALVES):
            all_of(RS, t, h, rs_out, n_rows - 1).wait_send()
            all_of(RIGHT, t, h, right, n_chip - 1).wait_send()
            all_of(AG, t, h, ag, n_rows - 1).wait_send()
            for j in range(CHUNKS):
                hop(t, h, j).wait_send()
        return 0

    lax.fori_loop(0, TICKS, drain, 0)


def on_device(inputs, weight, phases, labels, prediction, ridge_inverse, coefficients):
    n_rows = lax.axis_size("rows")
    n_feat = lax.axis_size("feat")
    n_y = 4
    rows = inputs.shape[0]
    fb = weight.shape[1]
    width = prediction.shape[1]
    strip = ridge_inverse.shape[0]
    hw = width // HALVES
    block = 2 * fb // n_rows
    cw = hw // 2
    scale = 1.0 / math.sqrt(rows * n_rows)
    bf = jnp.bfloat16
    vmem = pl.BlockSpec(memory_space=pltpu.VMEM)
    pieces = (TICKS, HALVES, n_rows, cw, block)
    return pl.pallas_call(
        functools.partial(kernel, n_rows, n_feat, n_y, scale),
        name="ridge",
        out_shape=(
            jax.ShapeDtypeStruct(coefficients.shape, jnp.float32),
            jax.ShapeDtypeStruct(prediction.shape, jnp.float32),
        ),
        in_specs=[vmem] * 7,
        out_specs=(vmem, vmem),
        scratch_shapes=[
            pltpu.VMEM((rows, fb), bf),
            pltpu.VMEM((TICKS + 1, width, rows), bf),
            pltpu.VMEM((TICKS + 1, HALVES, CHUNKS, hw, rows // CHUNKS), bf),
            pltpu.VMEM((hw, fb), jnp.float32),
            pltpu.VMEM(pieces, bf),
            pltpu.VMEM(pieces, bf),
            pltpu.VMEM((TICKS, HALVES, n_rows // 2, cw, block), bf),
            pltpu.VMEM(pieces, bf),
            pltpu.VMEM((TICKS, HALVES, CHUNKS, hw, rows // CHUNKS), bf),
            pltpu.VMEM((2, 2 * strip, fb), bf),
            pltpu.VMEM((TICKS, width, strip), jnp.float32),
            pltpu.SemaphoreType.DMA((3, TICKS, HALVES)),
            pltpu.SemaphoreType.DMA((3, TICKS, HALVES)),
            pltpu.SemaphoreType.DMA((TICKS, HALVES, CHUNKS)),
            pltpu.SemaphoreType.DMA((TICKS, HALVES, CHUNKS)),
            pltpu.SemaphoreType.DMA((TICKS + 1,)),
            pltpu.SemaphoreType.DMA((TICKS + 1,)),
            pltpu.SemaphoreType.DMA,
            pltpu.SemaphoreType.DMA,
        ],
        compiler_params=pltpu.CompilerParams(
            collective_id=0, has_side_effects=True, vmem_limit_bytes=60 * 2**20
        ),
    )(
        inputs,
        weight,
        phases.reshape(1, -1),
        labels.reshape(1, -1),
        prediction,
        ridge_inverse,
        coefficients,
    )


def solution(mesh):
    placed = (
        P("rows", None),
        P(None, "feat"),
        P("feat"),
        P("rows"),
        P("rows", "feat"),
        P(("feat", "rows"), None),
        P(("feat", "rows"), None),
    )
    return jax.shard_map(
        on_device,
        mesh=mesh,
        in_specs=placed,
        out_specs=(P(("feat", "rows"), None), P("rows", "feat")),
        check_vma=False,
    )
```

```python
import functools
import math

import jax
import jax.numpy as jnp
from jax import lax
from jax.experimental import pallas as pl
from jax.experimental.pallas import tpu as pltpu
from jax.sharding import PartitionSpec as P

TICKS = 4
RIDGE = 0.5
HALVES = 2
CHUNKS = 8

COS_POLY = (
    0.9999999890590228,
    -19.739204499453827,
    64.9391174598908,
    -85.45013953079768,
    60.16763095026347,
    -25.967599245923736,
    6.52865815775625,
)
INV_TURN = 1.0 / (2.0 * math.pi)

RS, RIGHT, AG = range(3)


def nt(a, b):
    return lax.dot_general(a, b, (((1,), (1,)), ((), ())), preferred_element_type=jnp.float32)


def kernel(
    n_rows, n_feat, n_y, scale,
    x_ref, w_ref, ph_ref, lab_ref, pred_ref, m_ref, c_ref,
    cout_ref, rout_ref,
    feat, preds, dsum, acc, m_own, rs_out, rs_in, right, ag, change, mcat, ctn,
    send, recv, hsend, hrecv, psend, precv, msend, mrecv, loads,
):
    me = lax.axis_index("rows")
    fi = lax.axis_index("feat")
    n_b = n_rows // n_y
    my_y = me // n_b
    my_b = lax.rem(me, n_b)
    sibling = me + 1 - 2 * lax.rem(me, 2)
    core = lax.rem(me, 2)
    chip = me // 2
    n_chip = n_rows // 2
    width = pred_ref.shape[1]
    rows = x_ref.shape[0]
    fb = w_ref.shape[1]
    strip = m_ref.shape[0]
    hw = width // HALVES
    cw = hw // 2
    block = fb // n_chip
    chunk = rows // CHUNKS
    nxt = lax.rem(fi + 1, n_feat)

    offsets = [(dy, db) for dy in (2, 1, 3, 0) for db in (2, 3, 1, 0)]

    def place(dy, db):
        return lax.rem(my_y + dy, n_y) * n_b + lax.rem(my_b + db, n_b)

    m_load = pltpu.make_async_copy(m_ref, m_own, loads.at[0])
    c_load = pltpu.make_async_copy(c_ref, cout_ref, loads.at[1])
    m_load.start()
    c_load.start()

    barrier = pltpu.get_barrier_semaphore()
    for dy, db in offsets[:-1]:
        pl.semaphore_signal(barrier, inc=1, device_id=(place(dy, db), fi))
    for k in (1, 2):
        pl.semaphore_signal(barrier, inc=1, device_id=(me, lax.rem(fi + k, n_feat)))
        pl.semaphore_signal(barrier, inc=1, device_id=(me, lax.rem(fi + n_feat - k, n_feat)))
    pl.semaphore_wait(barrier, n_rows - 1 + 4)

    own_rows = pl.ds(pl.multiple_of(core * strip, strip), strip)
    def turn(i, _):
        at = pl.ds(pl.multiple_of(i * 256, 256), 256)
        preds[0, :, at] = pred_ref[at, :].astype(jnp.float32).T.astype(jnp.bfloat16)
        return 0

    lax.fori_loop(0, rows // 256, turn, 0)

    def pred_copy(k):
        return pltpu.make_async_remote_copy(
            src_ref=preds.at[max(k - 2, 0)],
            dst_ref=preds.at[k],
            send_sem=psend.at[k],
            recv_sem=precv.at[k],
            device_id=(me, lax.rem(fi + min(k, 2), n_feat)),
        )

    pred_copy(1).start()
    pred_copy(2).start()

    tc = 256

    def featurise(i, _):
        c0 = pl.ds(pl.multiple_of(i * tc, tc), tc)
        linear = jnp.dot(x_ref[...], w_ref[:, c0], preferred_element_type=jnp.float32)
        turns = linear * INV_TURN + ph_ref[:, c0] * INV_TURN
        part = turns - jnp.round(turns)
        u = part * part
        value = u * (COS_POLY[-1] * scale) + COS_POLY[-2] * scale
        for a in COS_POLY[-3::-1]:
            value = value * u + a * scale
        feat[:, c0] = value.astype(jnp.bfloat16)
        return 0

    lax.fori_loop(0, fb // tc, featurise, 0)

    dsum[0] = jnp.zeros_like(dsum[0])

    def panel(t):
        return lax.rem(fi - t + n_feat, n_feat)

    def panel_columns(t):
        return pl.ds(pl.multiple_of(panel(t) * width, width), width)

    def residual(t, h, j):
        at = pl.ds(pl.multiple_of(j * chunk, chunk), chunk)
        cls = lax.broadcasted_iota(jnp.int32, (hw, chunk), 0) + (h * hw + panel(t) * width)
        hot = (lab_ref[:, at] == cls).astype(jnp.float32)
        return hot - preds[t, h * hw : (h + 1) * hw, at].astype(jnp.float32) - dsum[t, h, j].astype(jnp.float32)

    def to_place(kind, t, h, src, dst, device):
        return pltpu.make_async_remote_copy(
            src_ref=src,
            dst_ref=dst,
            send_sem=send.at[kind, t, h],
            recv_sem=recv.at[kind, t, h],
            device_id=(device, fi),
        )

    def all_of(kind, t, h, buf, count):
        some = buf.at[t, h, pl.ds(0, count)]
        return to_place(kind, t, h, some, some, sibling)

    def hop(t, h, j):
        return pltpu.make_async_remote_copy(
            src_ref=change.at[t, h, j],
            dst_ref=dsum.at[t + 1, h, j],
            send_sem=hsend.at[t, h, j],
            recv_sem=hrecv.at[t, h, j],
            device_id=(me, nxt),
        )

    def correlate(t, h):
        acc[...] = jnp.zeros_like(acc)
        cols = panel_columns(t)
        mine = pl.ds(pl.multiple_of(me * strip, strip), strip)
        acc[:, mine] = -RIDGE * cout_ref[:, cols].T[h * hw : (h + 1) * hw, :]

        def arrived(j):
            @pl.when(t > 0)
            def _():
                hop(t - 1, h, j).wait_recv()

            return residual(t, h, j).astype(jnp.bfloat16)

        def first(j, _):
            part = arrived(j)
            r0 = pl.ds(pl.multiple_of(j * chunk, chunk), chunk)
            acc[...] = acc[...] + jnp.dot(part, feat[r0, :], preferred_element_type=jnp.float32)
            return 0

        lax.fori_loop(0, CHUNKS - 1, first, 0)
        last = arrived(CHUNKS - 1)
        for dy in (2, 1, 3, 0):
            y = lax.rem(my_y + dy, n_y)
            c0 = pl.ds(pl.multiple_of(y * 2 * block, 2 * block), 2 * block)
            total = acc[:, c0] + jnp.dot(
                last, feat[rows - chunk : rows, c0], preferred_element_type=jnp.float32
            )
            total = total.astype(jnp.bfloat16)
            for b in range(n_b):
                lanes = slice(b // 2 * block, (b // 2 + 1) * block)
                rs_out[t, h, y * n_b + b] = total[b % 2 * cw : (b % 2 + 1) * cw, lanes]
            for db in (2, 3, 1, 0):
                if (dy, db) != (0, 0):
                    d = place(dy, db)
                    to_place(RS, t, h, rs_out.at[t, h, d], rs_in.at[t, h, me], d).start()
        rs_in[t, h, me] = rs_out[t, h, me]

    def collect(t, h):
        all_of(RS, t, h, rs_in, n_rows - 1).wait_recv()
        total = rs_in[t, h, 0].astype(jnp.float32)
        for s in range(1, n_rows):
            total = total + rs_in[t, h, s].astype(jnp.float32)
        right[t, h, chip] = total.astype(jnp.bfloat16)
        for dy, db in offsets[:-1]:
            if db % 2 == 0:
                mine = right.at[t, h, chip]
                to_place(RIGHT, t, h, mine, mine, place(dy, db)).start()

    def solve(t, h):
        all_of(RIGHT, t, h, right, n_chip - 1).wait_recv()
        whole = jnp.concatenate([right[t, h, a] for a in range(n_chip)], axis=1)
        own = nt(whole, mcat[0]) + nt(whole, mcat[1])
        ag[t, h, me] = own.astype(jnp.bfloat16)
        for dy, db in offsets[:-1]:
            to_place(AG, t, h, ag.at[t, h, me], ag.at[t, h, me], place(dy, db)).start()

    def update(t, h):
        all_of(AG, t, h, ag, n_rows - 1).wait_recv()
        delta = jnp.concatenate(
            [
                jnp.concatenate([ag[t, h, 2 * a + c] for a in range(n_chip)], axis=1)
                for c in range(2)
            ],
            axis=0,
        )

        def moved(j, _):
            at = pl.ds(pl.multiple_of(j * chunk, chunk), chunk)
            total = dsum[t, h, j].astype(jnp.float32) + nt(delta, feat[at, :])
            change[t, h, j] = total.astype(jnp.bfloat16)
            hop(t, h, j).start()
            return 0

        lax.fori_loop(0, CHUNKS, moved, 0)
        for c in range(2):
            lanes = slice(h * hw + c * cw, h * hw + (c + 1) * cw)
            ctn[t, lanes, :] = ag[t, h, 2 * chip + c, :, own_rows].astype(jnp.float32)

    c_load.wait()
    correlate(0, 0)
    correlate(0, 1)
    m_load.wait()
    high = m_own[...].astype(jnp.bfloat16)
    mcat[0, own_rows, :] = high
    mcat[1, own_rows, :] = (m_own[...] - high.astype(jnp.float32)).astype(jnp.bfloat16)
    ridge_copy = pltpu.make_async_remote_copy(
        src_ref=mcat.at[:, own_rows],
        dst_ref=mcat.at[:, own_rows],
        send_sem=msend,
        recv_sem=mrecv,
        device_id=(sibling, fi),
    )
    ridge_copy.start()
    ridge_copy.wait_recv()
    pred_copy(1).wait_recv()
    pred_copy(3).start()

    def tick(t, _):
        @pl.when(t == 2)
        def _():
            pred_copy(4).start()

        for h in range(HALVES):
            collect(t, h)
        for h in range(HALVES):
            solve(t, h)

        @pl.when(t == 1)
        def _():
            pred_copy(2).wait_recv()

        for h in range(HALVES):
            update(t, h)

        @pl.when(t == 2)
        def _():
            pred_copy(3).wait_recv()

        @pl.when(t < TICKS - 1)
        def _():
            for h in range(HALVES):
                correlate(t + 1, h)

        return 0

    lax.fori_loop(0, TICKS, tick, 0)

    for t in range(TICKS):
        cols = panel_columns(t)
        cout_ref[:, cols] = cout_ref[:, cols] + ctn[t].T

    pred_copy(TICKS).wait_recv()

    for j in range(CHUNKS):
        for h in range(HALVES):
            hop(TICKS - 1, h, j).wait_recv()
        parts = [residual(TICKS, h, j) for h in range(HALVES)]
        rout_ref[j * chunk : (j + 1) * chunk, :] = jnp.concatenate(parts, axis=0).T

    for k in range(1, TICKS + 1):
        pred_copy(k).wait_send()
    ridge_copy.wait_send()

    def drain(t, _):
        for h in range(HALVES):
            all_of(RS, t, h, rs_out, n_rows - 1).wait_send()
            all_of(RIGHT, t, h, right, n_chip - 1).wait_send()
            all_of(AG, t, h, ag, n_rows - 1).wait_send()
            for j in range(CHUNKS):
                hop(t, h, j).wait_send()
        return 0

    lax.fori_loop(0, TICKS, drain, 0)


def on_device(inputs, weight, phases, labels, prediction, ridge_inverse, coefficients):
    n_rows = lax.axis_size("rows")
    n_feat = lax.axis_size("feat")
    n_y = 4
    rows = inputs.shape[0]
    fb = weight.shape[1]
    width = prediction.shape[1]
    strip = ridge_inverse.shape[0]
    hw = width // HALVES
    block = 2 * fb // n_rows
    cw = hw // 2
    scale = 1.0 / math.sqrt(rows * n_rows)
    bf = jnp.bfloat16
    vmem = pl.BlockSpec(memory_space=pltpu.VMEM)
    pieces = (TICKS, HALVES, n_rows, cw, block)
    return pl.pallas_call(
        functools.partial(kernel, n_rows, n_feat, n_y, scale),
        name="ridge",
        out_shape=(
            jax.ShapeDtypeStruct(coefficients.shape, jnp.float32),
            jax.ShapeDtypeStruct(prediction.shape, jnp.float32),
        ),
        in_specs=[vmem] * 5 + [pl.BlockSpec(memory_space=pl.ANY)] * 2,
        out_specs=(vmem, vmem),
        scratch_shapes=[
            pltpu.VMEM((rows, fb), bf),
            pltpu.VMEM((TICKS + 1, width, rows), bf),
            pltpu.VMEM((TICKS + 1, HALVES, CHUNKS, hw, rows // CHUNKS), bf),
            pltpu.VMEM((hw, fb), jnp.float32),
            pltpu.VMEM((strip, fb), jnp.float32),
            pltpu.VMEM(pieces, bf),
            pltpu.VMEM(pieces, bf),
            pltpu.VMEM((TICKS, HALVES, n_rows // 2, cw, block), bf),
            pltpu.VMEM(pieces, bf),
            pltpu.VMEM((TICKS, HALVES, CHUNKS, hw, rows // CHUNKS), bf),
            pltpu.VMEM((2, 2 * strip, fb), bf),
            pltpu.VMEM((TICKS, width, strip), jnp.float32),
            pltpu.SemaphoreType.DMA((3, TICKS, HALVES)),
            pltpu.SemaphoreType.DMA((3, TICKS, HALVES)),
            pltpu.SemaphoreType.DMA((TICKS, HALVES, CHUNKS)),
            pltpu.SemaphoreType.DMA((TICKS, HALVES, CHUNKS)),
            pltpu.SemaphoreType.DMA((TICKS + 1,)),
            pltpu.SemaphoreType.DMA((TICKS + 1,)),
            pltpu.SemaphoreType.DMA,
            pltpu.SemaphoreType.DMA,
            pltpu.SemaphoreType.DMA((2,)),
        ],
        compiler_params=pltpu.CompilerParams(
            collective_id=0, has_side_effects=True, vmem_limit_bytes=60 * 2**20
        ),
    )(
        inputs,
        weight,
        phases.reshape(1, -1),
        labels.reshape(1, -1),
        prediction,
        ridge_inverse,
        coefficients,
    )


def solution(mesh):
    placed = (
        P("rows", None),
        P(None, "feat"),
        P("feat"),
        P("rows"),
        P("rows", "feat"),
        P(("feat", "rows"), None),
        P(("feat", "rows"), None),
    )
    return jax.shard_map(
        on_device,
        mesh=mesh,
        in_specs=placed,
        out_specs=(P(("feat", "rows"), None), P("rows", "feat")),
        check_vma=False,
    )
```

```python
import functools
import math

import jax
import jax.numpy as jnp
from jax import lax
from jax.experimental import pallas as pl
from jax.experimental.pallas import tpu as pltpu
from jax.sharding import PartitionSpec as P

TICKS = 4
RIDGE = 0.5
HALVES = 2
CHUNKS = 8

COS_POLY = (
    0.9999999890590228,
    -19.739204499453827,
    64.9391174598908,
    -85.45013953079768,
    60.16763095026347,
    -25.967599245923736,
    6.52865815775625,
)
INV_TURN = 1.0 / (2.0 * math.pi)

RS, RIGHT, AG = range(3)


def nt(a, b):
    return lax.dot_general(a, b, (((1,), (1,)), ((), ())), preferred_element_type=jnp.float32)


def kernel(
    n_rows, n_feat, n_y, scale,
    x_ref, w_ref, ph_ref, lab_ref, pred_ref, m_ref, c_ref,
    cout_ref, rout_ref,
    feat, preds, dsum, acc, m_own, rs_out, rs_in, right, ag, change, mcat, ctn,
    send, recv, hsend, hrecv, psend, precv, msend, mrecv, loads,
):
    me = lax.axis_index("rows")
    fi = lax.axis_index("feat")
    n_b = n_rows // n_y
    my_y = me // n_b
    my_b = lax.rem(me, n_b)
    sibling = me + 1 - 2 * lax.rem(me, 2)
    core = lax.rem(me, 2)
    chip = me // 2
    n_chip = n_rows // 2
    width = pred_ref.shape[1]
    rows = x_ref.shape[0]
    fb = w_ref.shape[1]
    strip = m_ref.shape[0]
    hw = width // HALVES
    cw = hw // 2
    block = fb // n_chip
    chunk = rows // CHUNKS
    nxt = lax.rem(fi + 1, n_feat)

    offsets = [(dy, db) for dy in (2, 1, 3, 0) for db in (2, 3, 1, 0)]

    def place(dy, db):
        return lax.rem(my_y + dy, n_y) * n_b + lax.rem(my_b + db, n_b)

    m_load = pltpu.make_async_copy(m_ref, m_own, loads.at[0])
    c_load = pltpu.make_async_copy(c_ref, cout_ref, loads.at[1])
    m_load.start()
    c_load.start()

    barrier = pltpu.get_barrier_semaphore()
    for dy, db in offsets[:-1]:
        pl.semaphore_signal(barrier, inc=1, device_id=(place(dy, db), fi))
    for k in (1, 2):
        pl.semaphore_signal(barrier, inc=1, device_id=(me, lax.rem(fi + k, n_feat)))
        pl.semaphore_signal(barrier, inc=1, device_id=(me, lax.rem(fi + n_feat - k, n_feat)))
    def turn(i, _):
        at = pl.ds(pl.multiple_of(i * 256, 256), 256)
        preds[0, :, at] = pred_ref[at, :].astype(jnp.float32).T.astype(jnp.bfloat16)
        return 0

    lax.fori_loop(0, rows // 256, turn, 0)

    pl.semaphore_wait(barrier, n_rows - 1 + 4)

    own_rows = pl.ds(pl.multiple_of(core * strip, strip), strip)
    def pred_copy(k):
        return pltpu.make_async_remote_copy(
            src_ref=preds.at[max(k - 2, 0)],
            dst_ref=preds.at[k],
            send_sem=psend.at[k],
            recv_sem=precv.at[k],
            device_id=(me, lax.rem(fi + min(k, 2), n_feat)),
        )

    pred_copy(1).start()
    pred_copy(2).start()

    tc = 256

    def featurise(i, _):
        c0 = pl.ds(pl.multiple_of(i * tc, tc), tc)
        linear = jnp.dot(x_ref[...], w_ref[:, c0], preferred_element_type=jnp.float32)
        turns = linear * INV_TURN + ph_ref[:, c0] * INV_TURN
        part = turns - jnp.round(turns)
        u = part * part
        value = u * (COS_POLY[-1] * scale) + COS_POLY[-2] * scale
        for a in COS_POLY[-3::-1]:
            value = value * u + a * scale
        feat[:, c0] = value.astype(jnp.bfloat16)
        return 0

    lax.fori_loop(0, fb // tc, featurise, 0)

    dsum[0] = jnp.zeros_like(dsum[0])

    def panel(t):
        return lax.rem(fi - t + n_feat, n_feat)

    def panel_columns(t):
        return pl.ds(pl.multiple_of(panel(t) * width, width), width)

    def residual(t, h, j):
        at = pl.ds(pl.multiple_of(j * chunk, chunk), chunk)
        cls = lax.broadcasted_iota(jnp.int32, (hw, chunk), 0) + (h * hw + panel(t) * width)
        hot = (lab_ref[:, at] == cls).astype(jnp.float32)
        return hot - preds[t, h * hw : (h + 1) * hw, at].astype(jnp.float32) - dsum[t, h, j].astype(jnp.float32)

    def to_place(kind, t, h, src, dst, device):
        return pltpu.make_async_remote_copy(
            src_ref=src,
            dst_ref=dst,
            send_sem=send.at[kind, t, h],
            recv_sem=recv.at[kind, t, h],
            device_id=(device, fi),
        )

    def all_of(kind, t, h, buf, count):
        some = buf.at[t, h, pl.ds(0, count)]
        return to_place(kind, t, h, some, some, sibling)

    def hop(t, h, j):
        return pltpu.make_async_remote_copy(
            src_ref=change.at[t, h, j],
            dst_ref=dsum.at[t + 1, h, j],
            send_sem=hsend.at[t, h, j],
            recv_sem=hrecv.at[t, h, j],
            device_id=(me, nxt),
        )

    def correlate(t, h):
        acc[...] = jnp.zeros_like(acc)
        cols = panel_columns(t)
        mine = pl.ds(pl.multiple_of(me * strip, strip), strip)
        acc[:, mine] = -RIDGE * cout_ref[:, cols].T[h * hw : (h + 1) * hw, :]

        def arrived(j):
            @pl.when(t > 0)
            def _():
                hop(t - 1, h, j).wait_recv()

            return residual(t, h, j).astype(jnp.bfloat16)

        def first(j, _):
            part = arrived(j)
            r0 = pl.ds(pl.multiple_of(j * chunk, chunk), chunk)
            acc[...] = acc[...] + jnp.dot(part, feat[r0, :], preferred_element_type=jnp.float32)
            return 0

        lax.fori_loop(0, CHUNKS - 1, first, 0)
        last = arrived(CHUNKS - 1)
        for dy in (2, 1, 3, 0):
            y = lax.rem(my_y + dy, n_y)
            c0 = pl.ds(pl.multiple_of(y * 2 * block, 2 * block), 2 * block)
            total = acc[:, c0] + jnp.dot(
                last, feat[rows - chunk : rows, c0], preferred_element_type=jnp.float32
            )
            total = total.astype(jnp.bfloat16)
            for b in range(n_b):
                lanes = slice(b // 2 * block, (b // 2 + 1) * block)
                rs_out[t, h, y * n_b + b] = total[b % 2 * cw : (b % 2 + 1) * cw, lanes]
            for db in (2, 3, 1, 0):
                if (dy, db) != (0, 0):
                    d = place(dy, db)
                    to_place(RS, t, h, rs_out.at[t, h, d], rs_in.at[t, h, me], d).start()
        rs_in[t, h, me] = rs_out[t, h, me]

    def collect(t, h):
        all_of(RS, t, h, rs_in, n_rows - 1).wait_recv()
        total = rs_in[t, h, 0].astype(jnp.float32)
        for s in range(1, n_rows):
            total = total + rs_in[t, h, s].astype(jnp.float32)
        right[t, h, chip] = total.astype(jnp.bfloat16)
        for dy, db in offsets[:-1]:
            if db % 2 == 0:
                mine = right.at[t, h, chip]
                to_place(RIGHT, t, h, mine, mine, place(dy, db)).start()

    def solve(t, h):
        all_of(RIGHT, t, h, right, n_chip - 1).wait_recv()
        whole = jnp.concatenate([right[t, h, a] for a in range(n_chip)], axis=1)
        own = nt(whole, mcat[0]) + nt(whole, mcat[1])
        ag[t, h, me] = own.astype(jnp.bfloat16)
        for dy, db in offsets[:-1]:
            to_place(AG, t, h, ag.at[t, h, me], ag.at[t, h, me], place(dy, db)).start()

    def update(t, h):
        all_of(AG, t, h, ag, n_rows - 1).wait_recv()
        delta = jnp.concatenate(
            [
                jnp.concatenate([ag[t, h, 2 * a + c] for a in range(n_chip)], axis=1)
                for c in range(2)
            ],
            axis=0,
        )

        def moved(j, _):
            at = pl.ds(pl.multiple_of(j * chunk, chunk), chunk)
            total = dsum[t, h, j].astype(jnp.float32) + nt(delta, feat[at, :])
            change[t, h, j] = total.astype(jnp.bfloat16)
            hop(t, h, j).start()
            return 0

        lax.fori_loop(0, CHUNKS, moved, 0)
        for c in range(2):
            lanes = slice(h * hw + c * cw, h * hw + (c + 1) * cw)
            ctn[t, lanes, :] = ag[t, h, 2 * chip + c, :, own_rows].astype(jnp.float32)

    c_load.wait()
    correlate(0, 0)
    correlate(0, 1)
    m_load.wait()
    high = m_own[...].astype(jnp.bfloat16)
    mcat[0, own_rows, :] = high
    mcat[1, own_rows, :] = (m_own[...] - high.astype(jnp.float32)).astype(jnp.bfloat16)
    ridge_copy = pltpu.make_async_remote_copy(
        src_ref=mcat.at[:, own_rows],
        dst_ref=mcat.at[:, own_rows],
        send_sem=msend,
        recv_sem=mrecv,
        device_id=(sibling, fi),
    )
    ridge_copy.start()
    ridge_copy.wait_recv()
    pred_copy(1).wait_recv()
    pred_copy(3).start()

    def tick(t, _):
        @pl.when(t == 2)
        def _():
            pred_copy(4).start()

        for h in range(HALVES):
            collect(t, h)
        for h in range(HALVES):
            solve(t, h)

        @pl.when(t == 1)
        def _():
            pred_copy(2).wait_recv()

        for h in range(HALVES):
            update(t, h)

        @pl.when(t == 2)
        def _():
            pred_copy(3).wait_recv()

        @pl.when(t < TICKS - 1)
        def _():
            for h in range(HALVES):
                correlate(t + 1, h)

        return 0

    lax.fori_loop(0, TICKS, tick, 0)

    for t in range(TICKS):
        cols = panel_columns(t)
        cout_ref[:, cols] = cout_ref[:, cols] + ctn[t].T

    pred_copy(TICKS).wait_recv()

    for j in range(CHUNKS):
        for h in range(HALVES):
            hop(TICKS - 1, h, j).wait_recv()
        parts = [residual(TICKS, h, j) for h in range(HALVES)]
        rout_ref[j * chunk : (j + 1) * chunk, :] = jnp.concatenate(parts, axis=0).T

    for k in range(1, TICKS + 1):
        pred_copy(k).wait_send()
    ridge_copy.wait_send()

    def drain(t, _):
        for h in range(HALVES):
            all_of(RS, t, h, rs_out, n_rows - 1).wait_send()
            all_of(RIGHT, t, h, right, n_chip - 1).wait_send()
            all_of(AG, t, h, ag, n_rows - 1).wait_send()
            for j in range(CHUNKS):
                hop(t, h, j).wait_send()
        return 0

    lax.fori_loop(0, TICKS, drain, 0)


def on_device(inputs, weight, phases, labels, prediction, ridge_inverse, coefficients):
    n_rows = lax.axis_size("rows")
    n_feat = lax.axis_size("feat")
    n_y = 4
    rows = inputs.shape[0]
    fb = weight.shape[1]
    width = prediction.shape[1]
    strip = ridge_inverse.shape[0]
    hw = width // HALVES
    block = 2 * fb // n_rows
    cw = hw // 2
    scale = 1.0 / math.sqrt(rows * n_rows)
    bf = jnp.bfloat16
    vmem = pl.BlockSpec(memory_space=pltpu.VMEM)
    pieces = (TICKS, HALVES, n_rows, cw, block)
    return pl.pallas_call(
        functools.partial(kernel, n_rows, n_feat, n_y, scale),
        name="ridge",
        out_shape=(
            jax.ShapeDtypeStruct(coefficients.shape, jnp.float32),
            jax.ShapeDtypeStruct(prediction.shape, jnp.float32),
        ),
        in_specs=[vmem] * 5 + [pl.BlockSpec(memory_space=pl.ANY)] * 2,
        out_specs=(vmem, vmem),
        scratch_shapes=[
            pltpu.VMEM((rows, fb), bf),
            pltpu.VMEM((TICKS + 1, width, rows), bf),
            pltpu.VMEM((TICKS + 1, HALVES, CHUNKS, hw, rows // CHUNKS), bf),
            pltpu.VMEM((hw, fb), jnp.float32),
            pltpu.VMEM((strip, fb), jnp.float32),
            pltpu.VMEM(pieces, bf),
            pltpu.VMEM(pieces, bf),
            pltpu.VMEM((TICKS, HALVES, n_rows // 2, cw, block), bf),
            pltpu.VMEM(pieces, bf),
            pltpu.VMEM((TICKS, HALVES, CHUNKS, hw, rows // CHUNKS), bf),
            pltpu.VMEM((2, 2 * strip, fb), bf),
            pltpu.VMEM((TICKS, width, strip), jnp.float32),
            pltpu.SemaphoreType.DMA((3, TICKS, HALVES)),
            pltpu.SemaphoreType.DMA((3, TICKS, HALVES)),
            pltpu.SemaphoreType.DMA((TICKS, HALVES, CHUNKS)),
            pltpu.SemaphoreType.DMA((TICKS, HALVES, CHUNKS)),
            pltpu.SemaphoreType.DMA((TICKS + 1,)),
            pltpu.SemaphoreType.DMA((TICKS + 1,)),
            pltpu.SemaphoreType.DMA,
            pltpu.SemaphoreType.DMA,
            pltpu.SemaphoreType.DMA((2,)),
        ],
        compiler_params=pltpu.CompilerParams(
            collective_id=0, has_side_effects=True, vmem_limit_bytes=60 * 2**20
        ),
    )(
        inputs,
        weight,
        phases.reshape(1, -1),
        labels.reshape(1, -1),
        prediction,
        ridge_inverse,
        coefficients,
    )


def solution(mesh):
    placed = (
        P("rows", None),
        P(None, "feat"),
        P("feat"),
        P("rows"),
        P("rows", "feat"),
        P(("feat", "rows"), None),
        P(("feat", "rows"), None),
    )
    return jax.shard_map(
        on_device,
        mesh=mesh,
        in_specs=placed,
        out_specs=(P(("feat", "rows"), None), P("rows", "feat")),
        check_vma=False,
    )
```
